256 devices in a mesh: tm: 16 (over x_lo, z), row: 4 (over y), col: 4 (over x_hi, core).
Axes of the slice: x: 4 (x_hi: 2, x_lo: 2; x = x_hi * 2 + x_lo), y: 4, z: 8, core: 2. Of those that a mesh axis runs over, the one named last changes fastest.
Arguments:
- resid: bfloat16 [16, 48, 160, 1152], P('tm', 'row', 'col'), may hold values from -8 to 8
- spatial_qkv: bfloat16 [3, 16, 48, 160, 1152], P(None, 'tm', 'row', 'col'), may hold values from -12 to 12
- key_keep: int32 [16, 48, 160], P('tm', 'row', 'col'), may hold values 0 or 1
- w_spatial_out: bfloat16 [1152, 1152], replicated, may hold values from -0.1875 to 0.1875
- modulation: float32 [2, 1152], replicated, may hold values from -3 to 3
- w_temporal_qkv: bfloat16 [1152, 3456], replicated, may hold values from -4 to 4
Outputs:
- temporal_heads: bfloat16 [16, 48, 160, 1152], P('tm', 'row', 'col')
The draws below stay inside these ranges and needn't reach their ends.
All inputs are finite; a program needn't handle non-finite values. No bound on the sum of `key_keep` on one device may be relied on, other than what follows from the above.
Results may differ from the reference program's by a relative error of at most 0.0084.
Values may be sent and summed in bfloat16 or wider, within the bound.
A program may use at most 128 MiB of HBM per device.

```python
import jax
import jax.numpy as jnp
from jax import lax

D = 1152
HEADS = 16
HEAD_DIM = 72
RADIUS = 3
FRAMES = 16
H = 48
W = 160


def draw_resid(key, part):
    values = jax.random.normal(key, (FRAMES, H, W, D), jnp.float32)
    return jnp.clip(values, -8.0, 8.0).astype(jnp.bfloat16)


def draw_spatial_qkv(key, part):
    first_key, second_key, third_key = jax.random.split(key, 3)
    shape_one = (FRAMES, H, W, D)
    queries_part = jnp.clip(jax.random.normal(first_key, shape_one, jnp.float32), -6.0, 6.0)
    keys_part = jnp.clip(jax.random.normal(second_key, shape_one, jnp.float32), -6.0, 6.0)
    values_part = jnp.clip(jax.random.normal(third_key, shape_one, jnp.float32), -6.0, 6.0)
    return jnp.stack([queries_part, keys_part, values_part], 0).astype(jnp.bfloat16)


def draw_w_temporal_qkv(key, part):
    first_key = jax.random.fold_in(key, 0)
    base = jax.random.normal(first_key, (D, 3 * D), jnp.float32) * D ** (-0.5)
    return jnp.clip(base, -4.0, 4.0).astype(jnp.bfloat16)


def touch_ends(values, stream_key, smallest, top_value):
    dims = values.shape
    index_at = [jax.random.randint(jax.random.fold_in(stream_key, axis), (), 0, dims[axis]) for axis in range(len(dims))]
    values = values.at[tuple(index_at)].set(smallest)
    longest = dims.index(max(dims))
    index_at[longest] = (index_at[longest] + 1) % dims[longest]
    return values.at[tuple(index_at)].set(top_value)


def gaussian(own_key, extent, deviation, reach, kind=jnp.bfloat16):
    return jnp.clip(deviation * jax.random.normal(own_key, extent, jnp.float32), -reach, reach).astype(kind)


def setup_inputs(seed: int = 0) -> dict:
    key_list = jax.random.split(jax.random.key(seed), 7)
    return {
        "resid": draw_resid(jax.random.fold_in(key_list[6], 71), 0),
        "spatial_qkv": draw_spatial_qkv(jax.random.fold_in(key_list[6], 71), 0),
        "key_keep": touch_ends((jax.random.randint(key_list[2], (FRAMES, H, W), 0, 16) < 13).astype(jnp.int32), jax.random.fold_in(key_list[2], 1), 0, 1),
        "w_spatial_out": gaussian(key_list[3], (D, D), D ** -0.5, 0.1875),
        "modulation": gaussian(key_list[4], (2, D), 0.5, 3.0, jnp.float32),
        "w_temporal_qkv": draw_w_temporal_qkv(jax.random.fold_in(key_list[6], 71), 0),
    }


NEG_FILL = -1e+30
EPSILON = 1e-06

def reference(resid, spatial_qkv, key_keep, w_spatial_out, modulation, w_temporal_qkv):
    score_scale = HEAD_DIM ** (-0.5)
    span = 2 * RADIUS + 1
    shape_heads = (H, W, HEADS, HEAD_DIM)
    padding = ((RADIUS, RADIUS), (RADIUS, RADIUS), (0, 0), (0, 0))

    def spatial_frame(frame):
        queries = spatial_qkv[0, frame].astype(jnp.float32).reshape(shape_heads)
        keys_pad = jnp.pad(spatial_qkv[1, frame].astype(jnp.float32).reshape(shape_heads), padding)
        values_pad = jnp.pad(spatial_qkv[2, frame].astype(jnp.float32).reshape(shape_heads), padding)
        keep_pad = jnp.pad(key_keep[frame], ((RADIUS, RADIUS), (RADIUS, RADIUS)))
        score_list = []
        allow_list = []
        for row_step in range(span):
            for col_step in range(span):
                key_slice = keys_pad[row_step:row_step + H, col_step:col_step + W]
                score_list.append(jnp.einsum('yxhd,yxhd->yxh', queries, key_slice) * score_scale)
                keep_slice = keep_pad[row_step:row_step + H, col_step:col_step + W] == 1
                if row_step == RADIUS and col_step == RADIUS:
                    keep_slice = jnp.ones_like(keep_slice)
                allow_list.append(keep_slice)
        scores = jnp.stack(score_list, -1)
        allowed = jnp.stack(allow_list, -1)[:, :, None, :]
        masked = jnp.where(allowed, scores, NEG_FILL)
        top_score = lax.optimization_barrier(jnp.max(masked, -1, keepdims=True))
        weights_f = jnp.where(allowed, jnp.exp(masked - top_score), 0.0)
        totals = lax.optimization_barrier(jnp.sum(weights_f, -1))
        weights_b = lax.optimization_barrier(weights_f.astype(jnp.bfloat16)).astype(jnp.float32)
        weighted = jnp.zeros(shape_heads, jnp.float32)
        for row_step in range(span):
            for col_step in range(span):
                position = row_step * span + col_step
                value_slice = values_pad[row_step:row_step + H, col_step:col_step + W]
                weighted = weighted + weights_b[..., position, None] * value_slice
        spatial_heads = (weighted / totals[..., None]).astype(jnp.bfloat16).reshape(H * W, D)
        stream = resid[frame].reshape(H * W, D).astype(jnp.float32) + jnp.dot(spatial_heads, w_spatial_out, preferred_element_type=jnp.float32)
        average = lax.optimization_barrier(jnp.mean(stream, -1, keepdims=True))
        centered = stream - average
        variance = lax.optimization_barrier(jnp.mean(centered * centered, -1, keepdims=True))
        normed = (centered * lax.rsqrt(variance + EPSILON) * (1.0 + modulation[1]) + modulation[0]).astype(jnp.bfloat16)
        return normed.reshape(H, W, D)
    normed_all = lax.map(spatial_frame, jnp.arange(FRAMES, dtype=jnp.int32))

    def temporal_row(row_index):
        block = lax.dynamic_index_in_dim(normed_all, row_index, 1, keepdims=False)
        projected = jnp.dot(block.reshape(FRAMES * W, D), w_temporal_qkv, preferred_element_type=jnp.float32).astype(jnp.bfloat16)
        projected = projected.reshape(FRAMES, W, 3, HEADS, HEAD_DIM).astype(jnp.float32)
        tscores = jnp.einsum('fphd,gphd->phfg', projected[:, :, 0], projected[:, :, 1]) * score_scale
        ttop = lax.optimization_barrier(jnp.max(tscores, -1, keepdims=True))
        tweights = jnp.exp(tscores - ttop)
        ttotals = lax.optimization_barrier(jnp.sum(tweights, -1))
        tweights_b = lax.optimization_barrier(tweights.astype(jnp.bfloat16)).astype(jnp.float32)
        tweighted = jnp.einsum('phfg,gphd->fphd', tweights_b, projected[:, :, 2])
        result = tweighted / jnp.transpose(ttotals, (2, 0, 1))[..., None]
        return result.astype(jnp.bfloat16).reshape(FRAMES, W, D)
    rows_out = lax.map(temporal_row, jnp.arange(H, dtype=jnp.int32))
    return jnp.transpose(rows_out, (1, 0, 2, 3))
```

```python
import jax
import jax.numpy as jnp
from jax import lax
from jax.sharding import PartitionSpec as P

HEADS = 16
RADIUS = 3


NEG_FILL = -1e30
EPSILON = 1e-06


def extended(array, sides, width):
    for axis, dim in sides:
        count, length = (lax.axis_size(axis), array.shape[dim])
        up = [(i, (i + 1) % count) for i in range(count - 1)]
        down = [(j, i) for i, j in up]
        last = lax.slice_in_dim(array, length - width, length, axis=dim)
        leading = lax.slice_in_dim(array, 0, width, axis=dim)
        before = lax.ppermute(last, axis, up)
        after = lax.ppermute(leading, axis, down)
        array = jnp.concatenate([before, array, after], axis=dim)
    return array


def softmax_parts(scores, allowed):
    masked = jnp.where(allowed, scores, NEG_FILL)
    top_score = jnp.max(masked, -1, keepdims=True)
    weights_f = jnp.where(allowed, jnp.exp(masked - top_score), 0.0)
    return (weights_f.astype(jnp.bfloat16), jnp.sum(weights_f, -1))


def frame_attend(gathered, head_count):
    frames_all, single, items, width_three = gathered.shape
    width = width_three // 3
    head_size = width // head_count
    split_qkv = gathered.reshape(frames_all, items, 3, head_count, head_size)
    scores = jnp.einsum(
        "fphd,gphd->phfg",
        split_qkv[:, :, 0],
        split_qkv[:, :, 1],
        preferred_element_type=jnp.float32,
    ) * head_size ** (-0.5)
    weights_b, totals = softmax_parts(scores, True)
    weighted = jnp.einsum(
        "phfg,gphd->fphd", weights_b, split_qkv[:, :, 2], preferred_element_type=jnp.float32
    )
    result = weighted / jnp.transpose(totals, (2, 0, 1))[..., None]
    return result.astype(jnp.bfloat16).reshape(frames_all, single, items, width)


def per_device(resid, spatial_qkv, key_keep, w_spatial_out, modulation, w_temporal_qkv):
    frame_count, tile_rows, tile_cols, width = resid.shape
    head_size = width // HEADS
    score_scale = head_size ** (-0.5)
    tile_tokens = tile_rows * tile_cols
    pair = spatial_qkv[1:3]
    keep_flags = key_keep.astype(jnp.bfloat16)[None, :, :, :, None]
    padded_pair, padded_keep = (
        extended(pair, (("row", 2), ("col", 3)), RADIUS),
        extended(keep_flags, (("row", 2), ("col", 3)), RADIUS),
    )
    pad_rows = tile_rows + 2 * RADIUS
    pad_cols = tile_cols + 2 * RADIUS
    key_count = pad_rows * pad_cols
    queries = spatial_qkv[0].reshape(frame_count, tile_tokens, HEADS, head_size)
    keys_pad = padded_pair[0].reshape(frame_count, key_count, HEADS, head_size)
    values_pad = padded_pair[1].reshape(frame_count, key_count, HEADS, head_size)
    query_index = jnp.arange(tile_tokens)
    query_row = query_index // tile_cols
    query_col = query_index % tile_cols
    key_index = jnp.arange(key_count)
    key_row = key_index // pad_cols
    key_col = key_index % pad_cols
    row_gap = key_row[None, :] - query_row[:, None] - RADIUS
    col_gap = key_col[None, :] - query_col[:, None] - RADIUS
    in_window = (jnp.abs(row_gap) <= RADIUS) & (jnp.abs(col_gap) <= RADIUS)
    itself = (row_gap == 0) & (col_gap == 0)
    key_live = padded_keep.reshape(frame_count, key_count) > 0.5
    allowed = (in_window[None] & (key_live[:, None, :] | itself[None]))[:, None]
    scores = (
        jnp.einsum("fqhd,fkhd->fhqk", queries, keys_pad, preferred_element_type=jnp.float32)
        * score_scale
    )
    weights_b, totals = softmax_parts(scores, allowed)
    weighted = jnp.einsum(
        "fhqk,fkhd->fqhd", weights_b, values_pad, preferred_element_type=jnp.float32
    )
    spatial_heads = (weighted / jnp.transpose(totals, (0, 2, 1))[..., None]).astype(jnp.bfloat16)
    spatial_heads = spatial_heads.reshape(frame_count * tile_tokens, width)
    stream = resid.reshape(frame_count * tile_tokens, width).astype(jnp.float32) + jnp.dot(
        spatial_heads, w_spatial_out, preferred_element_type=jnp.float32
    )
    average = jnp.mean(stream, -1, keepdims=True)
    centered = stream - average
    variance = jnp.mean(centered * centered, -1, keepdims=True)
    normed = (
        centered * lax.rsqrt(variance + EPSILON) * (1.0 + modulation[1]) + modulation[0]
    ).astype(jnp.bfloat16)
    tm_count = lax.axis_size("tm")
    part_tokens = tile_tokens // tm_count
    exchanged = lax.all_to_all(
        normed.reshape(frame_count, tm_count, part_tokens, width),
        "tm",
        split_axis=1,
        concat_axis=0,
        tiled=True,
    )
    projected = jnp.dot(
        exchanged.reshape(tm_count * part_tokens, width),
        w_temporal_qkv,
        preferred_element_type=jnp.float32,
    ).astype(jnp.bfloat16)
    projected = projected.reshape(tm_count, frame_count, part_tokens, 3 * width)
    result = lax.all_to_all(
        frame_attend(projected, HEADS), "tm", split_axis=0, concat_axis=1, tiled=True
    )
    return result.reshape(frame_count, tile_rows, tile_cols, width)


def solution(mesh):
    return jax.shard_map(
        per_device,
        mesh=mesh,
        in_specs=(
            P("tm", "row", "col", None),
            P(None, "tm", "row", "col", None),
            P("tm", "row", "col"),
            P(),
            P(),
            P(),
        ),
        out_specs=P("tm", "row", "col", None),
        check_vma=False,
    )
```

```python
import jax
import jax.numpy as jnp
from jax import lax
from jax.experimental import pallas as pl
from jax.experimental.pallas import tpu as pltpu
from jax.sharding import PartitionSpec as P

HEADS = 16
RADIUS = 3
NEG_FILL = -1e30
EPSILON = 1e-06
LOG2E = 1.4426950408889634
LANES = 128
UNIT = 8
MESH = pl.DeviceIdType.MESH


def head_windows(width, heads):
    size = width // heads
    last = width // LANES - 2
    found = {}
    for head in range(heads):
        tile = min(head * size // LANES, last)
        if (tile - 1) in found and (head + 1) * size <= (tile + 1) * LANES:
            tile = tile - 1
        found.setdefault(tile, []).append(head)
    return sorted(found.items())


def attend(query, key, value, bias, heads, tile, size, out_ref):
    factor = size ** (-0.5) * LOG2E
    lane = lax.broadcasted_iota(jnp.int32, (1, 2 * LANES), 1) + tile * LANES
    place = slice(tile * LANES, (tile + 2) * LANES)
    current = out_ref[:, place]
    for head in heads:
        inside = (lane >= head * size) & (lane < (head + 1) * size)
        chosen = query * jnp.where(inside, 1.0, 0.0).astype(jnp.bfloat16)
        scores = lax.dot_general(
            chosen, key, (((1,), (1,)), ((), ())), preferred_element_type=jnp.float32
        )
        scores = scores + bias[...]
        top = jnp.max(scores, -1, keepdims=True)
        weights = jnp.exp2((scores - top) * factor)
        total = jnp.sum(weights, -1, keepdims=True)
        mixed = jnp.dot(
            weights.astype(jnp.bfloat16), value, preferred_element_type=jnp.float32
        )
        current = jnp.where(inside, mixed * (1.0 / total), current)
    out_ref[:, place] = current


def block_kernel(
    qkv, flags, resid, w_out, modulation, w_qkv,
    out,
    kb, vb, qb, rb, wo, mo, wq, hb, sbias, swin, ns, nr, tq, tb, tbias, ts,
    load_sem, col_send, col_recv, row_send, row_recv, cor_send, cor_recv,
    p1_send, p1_recv, p2_send, p2_recv, own_sem,
):
    me, row, col = lax.axis_index("tm"), lax.axis_index("row"), lax.axis_index("col")
    tm_count, row_count, col_count = (lax.axis_size(a) for a in ("tm", "row", "col"))
    _, tile_rows, tile_cols, width = qkv.shape
    size = width // HEADS
    windows = head_windows(width, HEADS)
    blocks = ns.shape[0] // (tm_count - 1)
    units = tm_count - 1
    block_rows = tile_rows // blocks
    rows_q = block_rows * tile_cols
    span = block_rows + 2 * RADIUS
    wide = tile_cols + 2 * UNIT
    keys = span * wide
    low, high = tile_rows, tile_rows + RADIUS
    own_rows = pl.ds(RADIUS, tile_rows)

    loads = [
        pltpu.make_async_copy(qkv.at[1], kb.at[own_rows, pl.ds(0, tile_cols), pl.ds(0, width)], load_sem.at[0]),
        pltpu.make_async_copy(flags, kb.at[own_rows, pl.ds(0, tile_cols), pl.ds(width, LANES)], load_sem.at[1]),
        pltpu.make_async_copy(qkv.at[0], qb, load_sem.at[2]),
        pltpu.make_async_copy(qkv.at[2], vb.at[own_rows, pl.ds(0, tile_cols)], load_sem.at[3]),
        pltpu.make_async_copy(w_out, wo, load_sem.at[4]),
        pltpu.make_async_copy(resid, rb, load_sem.at[5]),
        pltpu.make_async_copy(modulation, mo, load_sem.at[6]),
        pltpu.make_async_copy(w_qkv, wq, load_sem.at[7]),
    ]
    for load in loads:
        load.start()

    barrier = pltpu.get_barrier_semaphore()

    def greet(step, carry):
        pl.semaphore_signal(barrier, inc=1, device_id={"tm": lax.rem(me + step, tm_count)}, device_id_type=MESH)
        return carry

    lax.fori_loop(1, tm_count, greet, 0)
    for step in (1, row_count - 1):
        pl.semaphore_signal(barrier, inc=1, device_id={"row": lax.rem(row + step, row_count)}, device_id_type=MESH)
    for step in (1, col_count - 1):
        pl.semaphore_signal(barrier, inc=1, device_id={"col": lax.rem(col + step, col_count)}, device_id_type=MESH)

    def clear(rows, cols):
        for buffer in (kb, vb):
            view = buffer.at[rows, cols]
            view[...] = jnp.zeros(view.shape, view.dtype)

    everything = pl.ds(0, tile_rows + 2 * RADIUS)
    pl.when(row == 0)(lambda: clear(pl.ds(0, RADIUS), pl.ds(0, wide)))
    pl.when(row == row_count - 1)(lambda: clear(pl.ds(low + RADIUS, RADIUS), pl.ds(0, wide)))
    pl.when(col == 0)(lambda: clear(everything, pl.ds(tile_cols, UNIT)))
    pl.when(col == col_count - 1)(lambda: clear(everything, pl.ds(tile_cols + UNIT, UNIT)))
    hb[...] = jnp.zeros_like(hb)
    tb[...] = jnp.zeros_like(tb)

    shape = (rows_q, keys)
    q_at = lax.broadcasted_iota(jnp.int32, shape, 0)
    k_at = lax.broadcasted_iota(jnp.int32, shape, 1)
    q_row = sum((q_at >= tile_cols * i).astype(jnp.int32) for i in range(1, block_rows))
    k_row = sum((k_at >= wide * i).astype(jnp.int32) for i in range(1, span))
    q_col = q_at - q_row * tile_cols
    k_col = k_at - k_row * wide
    k_col = jnp.where(
        k_col < tile_cols, k_col, jnp.where(k_col < tile_cols + UNIT, k_col - tile_cols - UNIT, k_col - UNIT)
    )
    row_gap, col_gap = k_row - q_row - RADIUS, k_col - q_col
    near = (jnp.abs(row_gap) <= RADIUS) & (jnp.abs(col_gap) <= RADIUS)
    itself = (row_gap == 0) & (col_gap == 0)
    swin[...] = jnp.where(near, 1.0, 0.0) + jnp.where(itself, 1.0, 0.0)
    t_shape = tbias.shape
    same = (
        lax.broadcasted_iota(jnp.int32, t_shape, 0) - lax.broadcasted_iota(jnp.int32, t_shape, 1)
    ) & (UNIT - 1)
    tbias[...] = jnp.where(same == 0, 0.0, NEG_FILL)

    pl.semaphore_wait(barrier, tm_count - 1 + 4)

    def halo(source_rows, source_cols, target_rows, target_cols, sends, recvs, target):
        copies = []
        for index, (array, buffer, lanes) in enumerate(
            ((qkv.at[1], kb, (0, width)), (flags, kb, (width, LANES)), (qkv.at[2], vb, (0, width)))
        ):
            copies.append(
                pltpu.make_async_remote_copy(
                    src_ref=array.at[source_rows, source_cols],
                    dst_ref=buffer.at[target_rows, target_cols, pl.ds(*lanes)],
                    send_sem=sends.at[index],
                    recv_sem=recvs.at[index],
                    device_id=target,
                    device_id_type=MESH,
                )
            )
        return copies

    def relay(source_cols, target_cols, rows, sends, recvs, target):
        return [
            pltpu.make_async_remote_copy(
                src_ref=buffer.at[rows, source_cols],
                dst_ref=buffer.at[rows, target_cols],
                send_sem=sends.at[index],
                recv_sem=recvs.at[index],
                device_id=target,
                device_id_type=MESH,
            )
            for index, buffer in enumerate((kb, vb))
        ]

    right = {"col": lax.rem(col + 1, col_count)}
    left = {"col": lax.rem(col + col_count - 1, col_count)}
    down = {"row": lax.rem(row + 1, row_count)}
    up = {"row": lax.rem(row + row_count - 1, row_count)}
    has = {
        "right": col < col_count - 1, "left": col > 0, "down": row < row_count - 1, "up": row > 0,
    }
    first_cols, last_cols = pl.ds(0, UNIT), pl.ds(tile_cols - UNIT, UNIT)
    left_strip, right_strip = pl.ds(tile_cols, UNIT), pl.ds(tile_cols + UNIT, UNIT)
    all_rows, all_cols = pl.ds(0, tile_rows), pl.ds(0, tile_cols)
    top_halo, bottom_halo = pl.ds(0, RADIUS), pl.ds(low + RADIUS, RADIUS)
    to_right = halo(all_rows, last_cols, own_rows, left_strip, col_send.at[0], col_recv.at[0], right)
    to_left = halo(all_rows, first_cols, own_rows, right_strip, col_send.at[1], col_recv.at[1], left)
    to_down = halo(pl.ds(tile_rows - RADIUS, RADIUS), all_cols, top_halo, all_cols, row_send.at[0], row_recv.at[0], down)
    to_up = halo(pl.ds(0, RADIUS), all_cols, bottom_halo, all_cols, row_send.at[1], row_recv.at[1], up)

    def start(copies):
        for copy in copies:
            copy.start()

    def got(copies):
        for copy in copies:
            copy.wait_recv()

    def sent(copies):
        for copy in copies:
            copy.wait_send()

    pl.when(has["right"])(lambda: start(to_right))
    pl.when(has["left"])(lambda: start(to_left))
    pl.when(has["down"])(lambda: start(to_down))
    pl.when(has["up"])(lambda: start(to_up))

    corners = []
    for index, (rows, row_side) in enumerate(((top_halo, "up"), (bottom_halo, "down"))):
        corners.append(
            (relay(last_cols, left_strip, rows, cor_send.at[index, 0], cor_recv.at[index, 0], right),
             has[row_side] & has["right"], has[row_side] & has["left"])
        )
        corners.append(
            (relay(first_cols, right_strip, rows, cor_send.at[index, 1], cor_recv.at[index, 1], left),
             has[row_side] & has["left"], has[row_side] & has["right"])
        )

    for load in loads[:4]:
        load.wait()
    pl.when(has["left"])(lambda: got(to_right))
    pl.when(has["right"])(lambda: got(to_left))

    def unit_of(block, device):
        return lax.rem(device - 4 * block + 4 * tm_count, tm_count)

    def first_copy(block, owner):
        return pltpu.make_async_remote_copy(
            src_ref=ns.at[block * units + unit_of(block, owner)],
            dst_ref=nr.at[block, me],
            send_sem=p1_send.at[block],
            recv_sem=p1_recv.at[block],
            device_id={"tm": owner},
            device_id_type=MESH,
        )

    def second_copy(block, unit, frame):
        return pltpu.make_async_remote_copy(
            src_ref=ts.at[block, frame],
            dst_ref=out.at[block * units + unit],
            send_sem=p2_send.at[block],
            recv_sem=p2_recv.at[block],
            device_id={"tm": frame},
            device_id_type=MESH,
        )

    def spatial(step, carry):
        block = lax.rem(step + 1, blocks)

        @pl.when(step == 1)
        def _():
            pl.when(has["up"])(lambda: got(to_down))
            pl.when(has["down"])(lambda: got(to_up))
            for copies, sends, _ in corners:
                pl.when(sends)(lambda copies=copies: start(copies))

        @pl.when(step == 2)
        def _():
            for copies, _, receives in corners:
                pl.when(receives)(lambda copies=copies: got(copies))

        first = block * block_rows
        lane = lax.broadcasted_iota(jnp.int32, (UNIT, LANES), 1)
        pick = jnp.where(lane == 0, 1.0, 0.0).astype(jnp.bfloat16)
        live = kb[pl.ds(first, span), :, width : width + LANES].reshape(keys, LANES)
        keep = lax.dot_general(pick, live, (((1,), (1,)), ((), ())), preferred_element_type=jnp.float32)
        sbias[...] = jnp.where(swin[...] + keep[0:1] > 1.5, 0.0, NEG_FILL)
        for tile, heads in windows:
            place = slice(tile * LANES, (tile + 2) * LANES)
            query = qb[pl.ds(first, block_rows), :, place].reshape(rows_q, 2 * LANES)
            key = kb[pl.ds(first, span), :, place].reshape(keys, 2 * LANES)
            value = vb[pl.ds(first, span), :, place].reshape(keys, 2 * LANES)
            attend(query, key, value, sbias, heads, tile, size, hb)

        @pl.when(step == 0)
        def _():
            for load in loads[4:7]:
                load.wait()

        stream = rb[pl.ds(first, block_rows)].reshape(rows_q, width).astype(jnp.float32) + jnp.dot(
            hb[...].astype(jnp.bfloat16), wo[...], preferred_element_type=jnp.float32
        )
        average = jnp.mean(stream, -1, keepdims=True)
        centered = stream - average
        variance = jnp.mean(centered * centered, -1, keepdims=True)
        normed = centered * lax.rsqrt(variance + EPSILON) * (1.0 + mo[1:2]) + mo[0:1]
        ns[pl.ds(block * units, units)] = normed.astype(jnp.bfloat16).reshape(units, UNIT, width)
        mine = unit_of(block, me)

        @pl.when(mine < units)
        def _():
            nr[block, me] = ns[block * units + mine]

        def send(offset, carry):
            owner = lax.rem(me + offset, tm_count)

            @pl.when(unit_of(block, owner) < units)
            def _():
                first_copy(block, owner).start()

            return carry

        lax.fori_loop(1, tm_count, send, 0)
        return carry

    lax.fori_loop(0, blocks, spatial, 0)
    loads[7].wait()

    def temporal(step, carry):
        block = lax.rem(step + 1, blocks)
        mine = unit_of(block, me)

        @pl.when(mine < units)
        def _():
            arrived = nr.at[block, pl.ds(0, units)]
            pltpu.make_async_copy(arrived, arrived, p1_recv.at[block]).wait()
            rows = nr[block].reshape(tm_count * UNIT, width)
            for part in range(9):
                place = slice(part * 3 * LANES, (part + 1) * 3 * LANES)
                tq[:, place] = jnp.dot(
                    rows, wq[:, place], preferred_element_type=jnp.float32
                ).astype(jnp.bfloat16)
            for tile, heads in windows:
                place = [slice(i * width + tile * LANES, i * width + (tile + 2) * LANES) for i in range(3)]
                attend(tq[:, place[0]], tq[:, place[1]], tq[:, place[2]], tbias, heads, tile, size, tb)
            ts[block] = tb[...].astype(jnp.bfloat16).reshape(tm_count, UNIT, width)
            pltpu.make_async_copy(ts.at[block, me], out.at[block * units + mine], own_sem.at[block]).start()

            def send(offset, carry):
                second_copy(block, mine, lax.rem(me + offset, tm_count)).start()
                return carry

            lax.fori_loop(1, tm_count, send, 0)

        return carry

    lax.fori_loop(0, blocks, temporal, 0)

    pl.when(has["right"])(lambda: sent(to_right))
    pl.when(has["left"])(lambda: sent(to_left))
    pl.when(has["down"])(lambda: sent(to_down))
    pl.when(has["up"])(lambda: sent(to_up))
    for copies, sends, _ in corners:
        pl.when(sends)(lambda copies=copies: sent(copies))

    def finish(block, carry):
        mine = unit_of(block, me)

        @pl.when(mine < units)
        def _():
            part, whole = pl.ds(0, units - 1), pl.ds(0, units)
            pltpu.make_async_copy(ns.at[part], ns.at[part], p1_send.at[block]).wait()
            pltpu.make_async_copy(ts.at[block, whole], ts.at[block, whole], p2_send.at[block]).wait()
            pltpu.make_async_copy(out.at[part], out.at[part], p2_recv.at[block]).wait()
            pltpu.make_async_copy(ts.at[block, me], out.at[block * units + mine], own_sem.at[block]).wait()

        @pl.when(mine >= units)
        def _():
            whole = pl.ds(0, units)
            pltpu.make_async_copy(ns.at[whole], ns.at[whole], p1_send.at[block]).wait()
            pltpu.make_async_copy(out.at[whole], out.at[whole], p2_recv.at[block]).wait()

        return carry

    lax.fori_loop(0, blocks, finish, 0)


def per_device(resid, spatial_qkv, key_keep, w_spatial_out, modulation, w_temporal_qkv):
    frame_count, tile_rows, tile_cols, width = resid.shape
    tm_count = lax.axis_size("tm")
    units = tile_rows * tile_cols // UNIT
    blocks = units // (tm_count - 1)
    block_rows = tile_rows // blocks
    rows_q = block_rows * tile_cols
    wide = tile_cols + 2 * UNIT
    pad_rows = tile_rows + 2 * RADIUS
    keys = (block_rows + 2 * RADIUS) * wide
    flags = jnp.broadcast_to(
        key_keep[0].astype(jnp.bfloat16)[..., None], (tile_rows, tile_cols, LANES)
    )
    bf16, f32 = jnp.bfloat16, jnp.float32
    dma = pltpu.SemaphoreType.DMA
    anywhere = pl.BlockSpec(memory_space=pl.ANY)
    result = pl.pallas_call(
        block_kernel,
        out_shape=jax.ShapeDtypeStruct((units, UNIT, width), bf16),
        in_specs=[anywhere] * 6,
        out_specs=anywhere,
        scratch_shapes=[
            pltpu.VMEM((pad_rows, wide, width + LANES), bf16),
            pltpu.VMEM((pad_rows, wide, width), bf16),
            pltpu.VMEM((tile_rows, tile_cols, width), bf16),
            pltpu.VMEM((tile_rows, tile_cols, width), bf16),
            pltpu.VMEM((width, width), bf16),
            pltpu.VMEM((2, width), f32),
            pltpu.VMEM((width, 3 * width), bf16),
            pltpu.VMEM((rows_q, width), f32),
            pltpu.VMEM((rows_q, keys), f32),
            pltpu.VMEM((rows_q, keys), f32),
            pltpu.VMEM((units, UNIT, width), bf16),
            pltpu.VMEM((blocks, tm_count, UNIT, width), bf16),
            pltpu.VMEM((tm_count * UNIT, 3 * width), bf16),
            pltpu.VMEM((tm_count * UNIT, width), f32),
            pltpu.VMEM((tm_count * UNIT, tm_count * UNIT), f32),
            pltpu.VMEM((blocks, tm_count, UNIT, width), bf16),
            dma((8,)),
            dma((2, 3)), dma((2, 3)), dma((2, 3)), dma((2, 3)), dma((2, 2, 2)), dma((2, 2, 2)),
            dma((blocks,)), dma((blocks,)), dma((blocks,)), dma((blocks,)), dma((blocks,)),
        ],
        compiler_params=pltpu.CompilerParams(
            collective_id=0, has_side_effects=True, vmem_limit_bytes=60 * 1024 * 1024
        ),
    )(
        spatial_qkv.reshape(3, tile_rows, tile_cols, width),
        flags,
        resid.reshape(tile_rows, tile_cols, width),
        w_spatial_out,
        modulation,
        w_temporal_qkv,
    )
    return result.reshape(frame_count, tile_rows, tile_cols, width)


def solution(mesh):
    return jax.shard_map(
        per_device,
        mesh=mesh,
        in_specs=(
            P("tm", "row", "col", None),
            P(None, "tm", "row", "col", None),
            P("tm", "row", "col"),
            P(),
            P(),
            P(),
        ),
        out_specs=P("tm", "row", "col", None),
        check_vma=False,
    )
```

```python
import jax
import jax.numpy as jnp
from jax import lax
from jax.experimental import pallas as pl
from jax.experimental.pallas import tpu as pltpu
from jax.sharding import PartitionSpec as P

HEADS = 16
RADIUS = 3
NEG_FILL = -1e30
EPSILON = 1e-06
LOG2E = 1.4426950408889634
LANES = 128
UNIT = 8
MESH = pl.DeviceIdType.MESH


def head_windows(width, heads):
    size = width // heads
    last = width // LANES - 2
    found = {}
    for head in range(heads):
        tile = min(head * size // LANES, last)
        if (tile - 1) in found and (head + 1) * size <= (tile + 1) * LANES:
            tile = tile - 1
        found.setdefault(tile, []).append(head)
    return sorted(found.items())


def attend(fetch, bias, windows, size, out_ref):
    factor = size ** (-0.5) * LOG2E
    lanes = 2 * LANES

    def masks(index):
        tile, heads = windows[index]
        lane = lax.broadcasted_iota(jnp.int32, (1, lanes), 1) + tile * LANES
        return [(lane >= head * size) & (lane < (head + 1) * size) for head in heads]

    def score(index):
        query, key = fetch(0, windows[index][0]), fetch(1, windows[index][0])
        chosen = [query * jnp.where(inside, 1.0, 0.0).astype(jnp.bfloat16) for inside in masks(index)]
        return lax.dot_general(
            jnp.concatenate(chosen, 0), key, (((1,), (1,)), ((), ())), preferred_element_type=jnp.float32
        )

    following = score(0)
    for index, (tile, heads) in enumerate(windows):
        scores = following
        if index + 1 < len(windows):
            following = score(index + 1)
        count = scores.shape[0] // len(heads)
        scores = scores.reshape(len(heads), count, -1) + bias[...][None]
        top = jnp.max(scores, -1, keepdims=True)
        weights = jnp.exp2((scores - top) * factor)
        total = jnp.sum(weights, -1, keepdims=True)
        mixed = jnp.dot(
            weights.reshape(len(heads) * count, -1).astype(jnp.bfloat16),
            fetch(2, tile),
            preferred_element_type=jnp.float32,
        ).reshape(len(heads), count, lanes) * (1.0 / total)
        place = slice(tile * LANES, tile * LANES + lanes)
        current = out_ref[0:count, place]
        for number, inside in enumerate(masks(index)):
            current = jnp.where(inside, mixed[number], current)
        out_ref[0:count, place] = current


def block_kernel(
    qkv, key_keep, resid, w_out, modulation, w_qkv,
    out,
    kk, flags, kb, vb, qb, rb, wo, mo, wq, hb, he, cbias, cwin, ebias, ewin, ns, nr, tq, tb, tbias, ts,
    load_sem, col_send, col_recv, row_send, row_recv, cor_send, cor_recv,
    p1_send, p1_recv, p2_send, p2_recv, own_sem,
):
    me, row, col = lax.axis_index("tm"), lax.axis_index("row"), lax.axis_index("col")
    tm_count, row_count, col_count = (lax.axis_size(a) for a in ("tm", "row", "col"))
    _, tile_rows, tile_cols, width = qkv.shape
    size = width // HEADS
    windows = head_windows(width, HEADS)
    units = ns.shape[0]
    rounds = nr.shape[0]
    groups = tile_cols // UNIT
    middle = groups - 2
    span = 3 * RADIUS
    wide = tile_cols + 2 * UNIT
    low = tile_rows
    many, few = RADIUS * middle, RADIUS * 2
    half = 2 * (many + few)
    core_cols = pl.ds(UNIT, tile_cols)
    own_rows = pl.ds(RADIUS, tile_rows)

    loads = [
        pltpu.make_async_copy(qkv.at[1], kb.at[own_rows, core_cols, pl.ds(0, width)], load_sem.at[0]),
        pltpu.make_async_copy(key_keep, kk, load_sem.at[1]),
        pltpu.make_async_copy(qkv.at[0], qb, load_sem.at[2]),
        pltpu.make_async_copy(qkv.at[2], vb.at[own_rows, core_cols], load_sem.at[3]),
        pltpu.make_async_copy(w_out, wo, load_sem.at[4]),
        pltpu.make_async_copy(resid, rb, load_sem.at[5]),
        pltpu.make_async_copy(modulation, mo, load_sem.at[6]),
        pltpu.make_async_copy(w_qkv, wq, load_sem.at[7]),
    ]
    for load in loads[:4]:
        load.start()

    barrier = pltpu.get_barrier_semaphore()

    def greet(step, carry):
        pl.semaphore_signal(barrier, inc=1, device_id={"tm": lax.rem(me + step, tm_count)}, device_id_type=MESH)
        return carry

    lax.fori_loop(1, tm_count, greet, 0)
    for step in (1, row_count - 1):
        pl.semaphore_signal(barrier, inc=1, device_id={"row": lax.rem(row + step, row_count)}, device_id_type=MESH)
    for step in (1, col_count - 1):
        pl.semaphore_signal(barrier, inc=1, device_id={"col": lax.rem(col + step, col_count)}, device_id_type=MESH)

    def clear(rows, cols):
        for buffer in (kb, vb):
            view = buffer.at[rows, cols]
            view[...] = jnp.zeros(view.shape, view.dtype)

    everything = pl.ds(0, tile_rows + 2 * RADIUS)
    pl.when(row == 0)(lambda: clear(pl.ds(0, RADIUS), pl.ds(0, wide)))
    pl.when(row == row_count - 1)(lambda: clear(pl.ds(low + RADIUS, RADIUS), pl.ds(0, wide)))
    pl.when(col == 0)(lambda: clear(everything, pl.ds(0, UNIT)))
    pl.when(col == col_count - 1)(lambda: clear(everything, pl.ds(tile_cols + UNIT, UNIT)))
    hb[...] = jnp.zeros_like(hb)
    he[...] = jnp.zeros_like(he)
    tb[...] = jnp.zeros_like(tb)

    def window(columns):
        shape = (RADIUS * columns, span * (columns + 2 * UNIT))
        q_at = lax.broadcasted_iota(jnp.int32, shape, 0)
        k_at = lax.broadcasted_iota(jnp.int32, shape, 1)
        q_row = sum((q_at >= columns * i).astype(jnp.int32) for i in range(1, RADIUS))
        k_row = sum((k_at >= (columns + 2 * UNIT) * i).astype(jnp.int32) for i in range(1, span))
        row_gap = k_row - q_row - RADIUS
        col_gap = k_at - k_row * (columns + 2 * UNIT) - UNIT - (q_at - q_row * columns)
        near = (jnp.abs(row_gap) <= RADIUS) & (jnp.abs(col_gap) <= RADIUS)
        itself = (row_gap == 0) & (col_gap == 0)
        return jnp.where(near, 1.0, 0.0) + jnp.where(itself, 1.0, 0.0)

    cwin[...] = window(middle * UNIT)
    ewin[...] = window(UNIT)
    t_shape = tbias.shape
    same = (
        lax.broadcasted_iota(jnp.int32, t_shape, 0) - lax.broadcasted_iota(jnp.int32, t_shape, 1)
    ) & (UNIT - 1)
    tbias[...] = jnp.where(same == 0, 0.0, NEG_FILL)


    def halo(source_rows, source_cols, target_rows, target_cols, sends, recvs, target):
        copies = []
        for index, (array, buffer, lanes) in enumerate(
            ((qkv.at[1], kb, (0, width)), (flags, kb, (width, LANES)), (qkv.at[2], vb, (0, width)))
        ):
            copies.append(
                pltpu.make_async_remote_copy(
                    src_ref=array.at[source_rows, source_cols],
                    dst_ref=buffer.at[target_rows, target_cols, pl.ds(*lanes)],
                    send_sem=sends.at[index],
                    recv_sem=recvs.at[index],
                    device_id=target,
                    device_id_type=MESH,
                )
            )
        return copies

    def relay(source_cols, target_cols, rows, sends, recvs, target):
        return [
            pltpu.make_async_remote_copy(
                src_ref=buffer.at[rows, source_cols],
                dst_ref=buffer.at[rows, target_cols],
                send_sem=sends.at[index],
                recv_sem=recvs.at[index],
                device_id=target,
                device_id_type=MESH,
            )
            for index, buffer in enumerate((kb, vb))
        ]

    right = {"col": lax.rem(col + 1, col_count)}
    left = {"col": lax.rem(col + col_count - 1, col_count)}
    down = {"row": lax.rem(row + 1, row_count)}
    up = {"row": lax.rem(row + row_count - 1, row_count)}
    has = {
        "right": col < col_count - 1, "left": col > 0, "down": row < row_count - 1, "up": row > 0,
    }
    first_cols, last_cols = pl.ds(0, UNIT), pl.ds(tile_cols - UNIT, UNIT)
    left_strip, right_strip = pl.ds(0, UNIT), pl.ds(tile_cols + UNIT, UNIT)
    own_first, own_last = pl.ds(UNIT, UNIT), pl.ds(tile_cols, UNIT)
    all_rows, all_cols = pl.ds(0, tile_rows), pl.ds(0, tile_cols)
    top_halo, bottom_halo = pl.ds(0, RADIUS), pl.ds(low + RADIUS, RADIUS)
    to_right = halo(all_rows, last_cols, own_rows, left_strip, col_send.at[0], col_recv.at[0], right)
    to_left = halo(all_rows, first_cols, own_rows, right_strip, col_send.at[1], col_recv.at[1], left)
    to_down = halo(pl.ds(tile_rows - RADIUS, RADIUS), all_cols, top_halo, core_cols, row_send.at[0], row_recv.at[0], down)
    to_up = halo(pl.ds(0, RADIUS), all_cols, bottom_halo, core_cols, row_send.at[1], row_recv.at[1], up)

    def start(copies):
        for copy in copies:
            copy.start()

    def got(copies):
        for copy in copies:
            copy.wait_recv()

    def sent(copies):
        for copy in copies:
            copy.wait_send()

    corners = []
    for index, (rows, row_side) in enumerate(((top_halo, "up"), (bottom_halo, "down"))):
        corners.append(
            (relay(own_last, left_strip, rows, cor_send.at[index, 0], cor_recv.at[index, 0], right),
             has[row_side] & has["right"], has[row_side] & has["left"])
        )
        corners.append(
            (relay(own_first, right_strip, rows, cor_send.at[index, 1], cor_recv.at[index, 1], left),
             has[row_side] & has["left"], has[row_side] & has["right"])
        )

    def owner_of(unit):
        return lax.rem(unit * 5, tm_count)

    def unit_of(turn):
        return turn * tm_count + lax.rem(me * 13, tm_count)

    def place_of(unit):
        step = unit // half
        rest = unit - step * half
        central = rest < 2 * many
        past = rest - 2 * many
        pick = jnp.where(central, rest // many, past // few)
        inner = jnp.where(central, lax.rem(rest, many), lax.rem(past + few, few))
        block = jnp.where(step == 0, 1 + pick, 3 * pick)
        line = jnp.where(central, inner // middle, lax.rem(inner, RADIUS))
        group = jnp.where(central, 1 + lax.rem(inner, middle), (groups - 1) * (inner // RADIUS))
        return (block * RADIUS + line) * groups + group

    def first_copy(unit, owner):
        return pltpu.make_async_remote_copy(
            src_ref=ns.at[unit],
            dst_ref=nr.at[unit // tm_count, me],
            send_sem=p1_send,
            recv_sem=p1_recv.at[unit // tm_count],
            device_id={"tm": owner},
            device_id_type=MESH,
        )

    def second_copy(turn, unit, frame):
        return pltpu.make_async_remote_copy(
            src_ref=ts.at[turn, frame],
            dst_ref=out.at[place_of(unit)],
            send_sem=p2_send,
            recv_sem=p2_recv,
            device_id={"tm": frame},
            device_id_type=MESH,
        )

    def bias_of(live, marks):
        lane = lax.broadcasted_iota(jnp.int32, (UNIT, LANES), 1)
        pick = jnp.where(lane == 0, 1.0, 0.0).astype(jnp.bfloat16)
        keep = lax.dot_general(pick, live, (((1,), (1,)), ((), ())), preferred_element_type=jnp.float32)
        return jnp.where(marks[...] + keep[0:1] > 1.5, 0.0, NEG_FILL)

    def look(block, start_col, columns, bias, marks, target):
        first = block * RADIUS
        spread = columns + 2 * UNIT

        def fetch(kind, tile):
            lanes = slice(tile * LANES, (tile + 2) * LANES)
            if kind == 0:
                return qb[pl.ds(first, RADIUS), start_col : start_col + columns, lanes].reshape(RADIUS * columns, 2 * LANES)
            buffer = kb if kind == 1 else vb
            return buffer[pl.ds(first, span), start_col : start_col + spread, lanes].reshape(span * spread, 2 * LANES)

        live = kb[pl.ds(first, span), start_col : start_col + spread, width : width + LANES].reshape(span * spread, LANES)
        bias[...] = bias_of(live, marks)
        attend(fetch, bias, windows, size, target)

    def emit(start_unit, count, base, heads):
        stream = base.astype(jnp.float32) + jnp.dot(
            heads.astype(jnp.bfloat16), wo[...], preferred_element_type=jnp.float32
        )
        average = jnp.mean(stream, -1, keepdims=True)
        centered = stream - average
        variance = jnp.mean(centered * centered, -1, keepdims=True)
        normed = centered * lax.rsqrt(variance + EPSILON) * (1.0 + mo[1:2]) + mo[0:1]
        ns[pl.ds(start_unit, count)] = normed.astype(jnp.bfloat16).reshape(count, UNIT, width)

        def send(index, carry):
            unit = start_unit + lax.rem(index + me, count)
            owner = owner_of(unit)

            @pl.when(owner == me)
            def _():
                nr[unit // tm_count, me] = ns[unit]

            @pl.when(owner != me)
            def _():
                first_copy(unit, owner).start()

            return carry

        lax.fori_loop(0, count, send, 0)

    def temporal(turn):
        unit = unit_of(turn)

        @pl.when(unit < units)
        def _():
            arrived = nr.at[turn, pl.ds(0, tm_count - 1)]
            pltpu.make_async_copy(arrived, arrived, p1_recv.at[turn]).wait()
            rows = nr[turn].reshape(tm_count * UNIT, width)
            for part in range(9):
                place = slice(part * 3 * LANES, (part + 1) * 3 * LANES)
                tq[:, place] = jnp.dot(
                    rows, wq[:, place], preferred_element_type=jnp.float32
                ).astype(jnp.bfloat16)

            def fetch(kind, tile):
                return tq[:, kind * width + tile * LANES : kind * width + (tile + 2) * LANES]

            attend(fetch, tbias, windows, size, tb)
            ts[turn] = tb[...].astype(jnp.bfloat16).reshape(tm_count, UNIT, width)
            pltpu.make_async_copy(ts.at[turn, me], out.at[place_of(unit)], own_sem.at[turn]).start()

            def send(offset, carry):
                second_copy(turn, unit, lax.rem(me + offset, tm_count)).start()
                return carry

            lax.fori_loop(1, tm_count, send, 0)

    for load in loads[4:7]:
        load.start()
    loads[1].wait()
    eye_shape = (tile_rows, tile_cols, tile_cols)
    diagonal = lax.broadcasted_iota(jnp.int32, eye_shape, 1) == lax.broadcasted_iota(jnp.int32, eye_shape, 2)
    spread_keep = jnp.where(diagonal, kk[...].astype(jnp.float32), 0.0).reshape(tile_rows * tile_cols, tile_cols)
    along = jnp.dot(
        spread_keep.astype(jnp.bfloat16),
        jnp.ones((tile_cols, LANES), jnp.bfloat16),
        preferred_element_type=jnp.float32,
    ).astype(jnp.bfloat16).reshape(tile_rows, tile_cols, LANES)
    flags[...] = along
    kb[own_rows, UNIT : UNIT + tile_cols, width : width + LANES] = along
    pl.semaphore_wait(barrier, tm_count - 1 + 4)
    pl.when(has["right"])(lambda: start(to_right))
    pl.when(has["left"])(lambda: start(to_left))
    pl.when(has["down"])(lambda: start(to_down))
    pl.when(has["up"])(lambda: start(to_up))
    loads[7].start()
    for index in (0, 2, 3):
        loads[index].wait()

    def step_body(step, carry):
        @pl.when(step == 1)
        def _():
            pl.when(has["up"])(lambda: got(to_down))
            pl.when(has["down"])(lambda: got(to_up))
            for copies, sends, _ in corners:
                pl.when(sends)(lambda copies=copies: start(copies))

        def centre(pick, carry):
            block = jnp.where(step == 0, 1 + pick, 3 * pick)
            look(block, UNIT, middle * UNIT, cbias, cwin, hb)

            @pl.when((step == 0) & (pick == 0))
            def _():
                for load in loads[4:7]:
                    load.wait()

            rows = middle * UNIT * RADIUS
            base = rb[pl.ds(block * RADIUS, RADIUS), UNIT : (middle + 1) * UNIT].reshape(rows, width)
            emit(step * half + pick * many, many, base, hb[...])
            return carry

        lax.fori_loop(0, 2, centre, 0)

        @pl.when(step == 0)
        def _():
            pl.when(has["left"])(lambda: got(to_right))
            pl.when(has["right"])(lambda: got(to_left))

        @pl.when(step == 1)
        def _():
            for copies, _, receives in corners:
                pl.when(receives)(lambda copies=copies: got(copies))

        def edge(pick, carry):
            block = jnp.where(step == 0, 1 + pick, 3 * pick)
            look(block, 0, UNIT, ebias, ewin, he.at[0])
            look(block, tile_cols - UNIT, UNIT, ebias, ewin, he.at[1])
            rows = UNIT * RADIUS
            lines = pl.ds(block * RADIUS, RADIUS)
            base = jnp.concatenate(
                [rb[lines, 0:UNIT].astype(jnp.float32).reshape(rows, width),
                 rb[lines, tile_cols - UNIT : tile_cols].astype(jnp.float32).reshape(rows, width)], 0
            )
            emit(step * half + 2 * many + pick * few, few, base, he[...].reshape(2 * rows, width))
            return carry

        lax.fori_loop(0, 2, edge, 0)
        pl.when(step == 0)(lambda: loads[7].wait())

        def turns(index, carry):
            temporal(index)
            return carry

        lax.fori_loop(step, 1 + step * (rounds - 1), turns, 0)
        return carry

    lax.fori_loop(0, 2, step_body, 0)

    pl.when(has["right"])(lambda: sent(to_right))
    pl.when(has["left"])(lambda: sent(to_left))
    pl.when(has["down"])(lambda: sent(to_down))
    pl.when(has["up"])(lambda: sent(to_up))
    for copies, sends, _ in corners:
        pl.when(sends)(lambda copies=copies: sent(copies))

    def settle(own):
        away = pl.ds(0, units - own)
        pltpu.make_async_copy(ns.at[away], ns.at[away], p1_send).wait()
        for turn in range(own):
            pltpu.make_async_copy(ts.at[turn, me], out.at[place_of(unit_of(turn))], own_sem.at[turn]).wait()
        spent = ts.at[pl.ds(0, own), pl.ds(0, tm_count - 1)]
        pltpu.make_async_copy(spent, spent, p2_send).wait()
        pltpu.make_async_copy(out.at[away], out.at[away], p2_recv).wait()

    pl.when(unit_of(rounds - 1) < units)(lambda: settle(rounds))
    pl.when(unit_of(rounds - 1) >= units)(lambda: settle(rounds - 1))


def per_device(resid, spatial_qkv, key_keep, w_spatial_out, modulation, w_temporal_qkv):
    frame_count, tile_rows, tile_cols, width = resid.shape
    tm_count = lax.axis_size("tm")
    units = tile_rows * tile_cols // UNIT
    rounds = -(-units // tm_count)
    columns = tile_cols - 2 * UNIT
    core_rows, edge_rows = RADIUS * columns, RADIUS * UNIT
    core_keys, edge_keys = 3 * RADIUS * tile_cols, 3 * RADIUS * 3 * UNIT
    wide = tile_cols + 2 * UNIT
    pad_rows = tile_rows + 2 * RADIUS
    bf16, f32 = jnp.bfloat16, jnp.float32
    dma = pltpu.SemaphoreType.DMA
    result = pl.pallas_call(
        block_kernel,
        out_shape=jax.ShapeDtypeStruct((units, UNIT, width), bf16),
        in_specs=[pl.BlockSpec(memory_space=pltpu.HBM)] * 6,
        out_specs=pl.BlockSpec(memory_space=pl.ANY),
        scratch_shapes=[
            pltpu.VMEM((tile_rows, 1, tile_cols), jnp.int32),
            pltpu.VMEM((tile_rows, tile_cols, LANES), bf16),
            pltpu.VMEM((pad_rows, wide, width + LANES), bf16),
            pltpu.VMEM((pad_rows, wide, width), bf16),
            pltpu.VMEM((tile_rows, tile_cols, width), bf16),
            pltpu.VMEM((tile_rows, tile_cols, width), bf16),
            pltpu.VMEM((width, width), bf16),
            pltpu.VMEM((2, width), f32),
            pltpu.VMEM((width, 3 * width), bf16),
            pltpu.VMEM((core_rows, width), f32),
            pltpu.VMEM((2, edge_rows, width), f32),
            pltpu.VMEM((core_rows, core_keys), f32),
            pltpu.VMEM((core_rows, core_keys), f32),
            pltpu.VMEM((edge_rows, edge_keys), f32),
            pltpu.VMEM((edge_rows, edge_keys), f32),
            pltpu.VMEM((units, UNIT, width), bf16),
            pltpu.VMEM((rounds, tm_count, UNIT, width), bf16),
            pltpu.VMEM((tm_count * UNIT, 3 * width), bf16),
            pltpu.VMEM((tm_count * UNIT, width), f32),
            pltpu.VMEM((tm_count * UNIT, tm_count * UNIT), f32),
            pltpu.VMEM((rounds, tm_count, UNIT, width), bf16),
            dma((8,)),
            dma((2, 3)), dma((2, 3)), dma((2, 3)), dma((2, 3)), dma((2, 2, 2)), dma((2, 2, 2)),
            dma, dma((rounds,)), dma, dma, dma((rounds,)),
        ],
        compiler_params=pltpu.CompilerParams(
            collective_id=0, has_side_effects=True, vmem_limit_bytes=58 * 1024 * 1024
        ),
    )(
        spatial_qkv.reshape(3, tile_rows, tile_cols, width),
        key_keep.reshape(tile_rows, 1, tile_cols),
        resid.reshape(tile_rows, tile_cols, width),
        w_spatial_out,
        modulation,
        w_temporal_qkv,
    )
    return result.reshape(frame_count, tile_rows, tile_cols, width)


def solution(mesh):
    return jax.shard_map(
        per_device,
        mesh=mesh,
        in_specs=(
            P("tm", "row", "col", None),
            P(None, "tm", "row", "col", None),
            P("tm", "row", "col"),
            P(),
            P(),
            P(),
        ),
        out_specs=P("tm", "row", "col", None),
        check_vma=False,
    )
```

```python
import jax
import jax.numpy as jnp
from jax import lax
from jax.experimental import pallas as pl
from jax.experimental.pallas import tpu as pltpu
from jax.sharding import PartitionSpec as P

HEADS = 16
RADIUS = 3
NEG_FILL = -1e30
EPSILON = 1e-06
LOG2E = 1.4426950408889634
LANES = 128
UNIT = 8
MESH = pl.DeviceIdType.MESH


def head_windows(width, heads):
    size = width // heads
    last = width // LANES - 2
    found = {}
    for head in range(heads):
        tile = min(head * size // LANES, last)
        if (tile - 1) in found and (head + 1) * size <= (tile + 1) * LANES:
            tile = tile - 1
        found.setdefault(tile, []).append(head)
    return sorted(found.items())


def far_first(count):
    ring = count // 2
    return sorted(range(1, count), key=lambda step: -(min(step % ring, ring - step % ring) * 2 + step // ring))


def attend(fetch, bias, windows, size, out_ref):
    factor = size ** (-0.5) * LOG2E
    lanes = 2 * LANES

    def masks(index):
        tile, heads = windows[index]
        lane = lax.broadcasted_iota(jnp.int32, (1, lanes), 1) + tile * LANES
        return [(lane >= head * size) & (lane < (head + 1) * size) for head in heads]

    def score(index):
        query, key = fetch(0, windows[index][0]), fetch(1, windows[index][0])
        chosen = [query * jnp.where(inside, 1.0, 0.0).astype(jnp.bfloat16) for inside in masks(index)]
        return lax.dot_general(
            jnp.concatenate(chosen, 0), key, (((1,), (1,)), ((), ())), preferred_element_type=jnp.float32
        )

    following = score(0)
    for index, (tile, heads) in enumerate(windows):
        scores = following
        if index + 1 < len(windows):
            following = score(index + 1)
        count = scores.shape[0] // len(heads)
        scores = scores.reshape(len(heads), count, -1) + bias[...][None]
        top = jnp.max(scores, -1, keepdims=True)
        weights = jnp.exp2((scores - top) * factor)
        total = jnp.sum(weights, -1, keepdims=True)
        mixed = jnp.dot(
            weights.reshape(len(heads) * count, -1).astype(jnp.bfloat16),
            fetch(2, tile),
            preferred_element_type=jnp.float32,
        ).reshape(len(heads), count, lanes) * (1.0 / total)
        place = slice(tile * LANES, tile * LANES + lanes)
        current = out_ref[0:count, place]
        for number, inside in enumerate(masks(index)):
            current = jnp.where(inside, mixed[number], current)
        out_ref[0:count, place] = current


def block_kernel(
    qkv, key_keep, resid, w_out, modulation, w_qkv,
    out,
    kk, flags, pack_cols, pack_cors, kb, vb, qb, rb, wo, mo, wq, hb, he, cbias, cwin, ebias, ewin, ns, nr, tq, tb, tbias, ts,
    load_sem, col_send, col_recv, row_send, row_recv, cor_send, cor_recv,
    p1_send, p1_recv, p2_send, p2_recv, own_sem,
):
    me, row, col = lax.axis_index("tm"), lax.axis_index("row"), lax.axis_index("col")
    tm_count, row_count, col_count = (lax.axis_size(a) for a in ("tm", "row", "col"))
    _, tile_rows, tile_cols, width = qkv.shape
    size = width // HEADS
    windows = head_windows(width, HEADS)
    units = ns.shape[0]
    rounds = nr.shape[0]
    groups = tile_cols // UNIT
    middle = groups - 2
    span = 3 * RADIUS
    wide = tile_cols + 2 * UNIT
    low = tile_rows
    many, few = RADIUS * middle, RADIUS * 2
    half = 2 * (many + few)
    core_cols = pl.ds(UNIT, tile_cols)
    own_rows = pl.ds(RADIUS, tile_rows)

    loads = [
        pltpu.make_async_copy(qkv.at[1], kb.at[own_rows, core_cols, pl.ds(0, width)], load_sem.at[0]),
        pltpu.make_async_copy(key_keep, kk, load_sem.at[1]),
        pltpu.make_async_copy(qkv.at[0], qb, load_sem.at[2]),
        pltpu.make_async_copy(qkv.at[2], vb.at[own_rows, core_cols], load_sem.at[3]),
        pltpu.make_async_copy(w_out, wo, load_sem.at[4]),
        pltpu.make_async_copy(resid, rb, load_sem.at[5]),
        pltpu.make_async_copy(modulation, mo, load_sem.at[6]),
        pltpu.make_async_copy(w_qkv, wq, load_sem.at[7]),
    ]
    for load in loads[:4]:
        load.start()

    barrier = pltpu.get_barrier_semaphore()

    def greet(step, carry):
        pl.semaphore_signal(barrier, inc=1, device_id={"tm": lax.rem(me + step, tm_count)}, device_id_type=MESH)
        return carry

    lax.fori_loop(1, tm_count, greet, 0)
    for step in (1, row_count - 1):
        pl.semaphore_signal(barrier, inc=1, device_id={"row": lax.rem(row + step, row_count)}, device_id_type=MESH)
    for step in (1, col_count - 1):
        pl.semaphore_signal(barrier, inc=1, device_id={"col": lax.rem(col + step, col_count)}, device_id_type=MESH)

    def clear(rows, cols):
        for buffer in (kb, vb):
            view = buffer.at[rows, cols]
            view[...] = jnp.zeros(view.shape, view.dtype)

    everything = pl.ds(0, tile_rows + 2 * RADIUS)
    pl.when(row == 0)(lambda: clear(pl.ds(0, RADIUS), pl.ds(0, wide)))
    pl.when(row == row_count - 1)(lambda: clear(pl.ds(low + RADIUS, RADIUS), pl.ds(0, wide)))
    pl.when(col == 0)(lambda: clear(everything, pl.ds(0, UNIT)))
    pl.when(col == col_count - 1)(lambda: clear(everything, pl.ds(tile_cols + UNIT, UNIT)))
    hb[...] = jnp.zeros_like(hb)
    he[...] = jnp.zeros_like(he)
    tb[...] = jnp.zeros_like(tb)

    def window(columns):
        shape = (RADIUS * columns, span * (columns + 2 * UNIT))
        q_at = lax.broadcasted_iota(jnp.int32, shape, 0)
        k_at = lax.broadcasted_iota(jnp.int32, shape, 1)
        q_row = sum((q_at >= columns * i).astype(jnp.int32) for i in range(1, RADIUS))
        k_row = sum((k_at >= (columns + 2 * UNIT) * i).astype(jnp.int32) for i in range(1, span))
        row_gap = k_row - q_row - RADIUS
        col_gap = k_at - k_row * (columns + 2 * UNIT) - UNIT - (q_at - q_row * columns)
        near = (jnp.abs(row_gap) <= RADIUS) & (jnp.abs(col_gap) <= RADIUS)
        itself = (row_gap == 0) & (col_gap == 0)
        return jnp.where(near, 1.0, 0.0) + jnp.where(itself, 1.0, 0.0)

    cwin[...] = window(middle * UNIT)
    ewin[...] = window(UNIT)
    t_shape = tbias.shape
    same = (
        lax.broadcasted_iota(jnp.int32, t_shape, 0) - lax.broadcasted_iota(jnp.int32, t_shape, 1)
    ) & (UNIT - 1)
    tbias[...] = jnp.where(same == 0, 0.0, NEG_FILL)


    def halo(source_rows, source_cols, target_rows, target_cols, sends, recvs, target):
        copies = []
        for index, (array, buffer, lanes) in enumerate(
            ((qkv.at[1], kb, (0, width)), (flags, kb, (width, LANES)), (qkv.at[2], vb, (0, width)))
        ):
            copies.append(
                pltpu.make_async_remote_copy(
                    src_ref=array.at[source_rows, source_cols],
                    dst_ref=buffer.at[target_rows, target_cols, pl.ds(*lanes)],
                    send_sem=sends.at[index],
                    recv_sem=recvs.at[index],
                    device_id=target,
                    device_id_type=MESH,
                )
            )
        return copies

    def pack(rows, cols, leading, target):
        keys = kb[rows, cols, 0:width].astype(jnp.float32)
        values = pltpu.roll(vb[rows, cols].astype(jnp.float32), 4, 1)
        line = lax.broadcasted_iota(jnp.int32, keys.shape, 1)
        wanted = (line < RADIUS) if leading else (line >= UNIT - RADIUS)
        target[:, :, 0:width] = jnp.where(wanted, keys, values).astype(jnp.bfloat16)
        target[:, :, width : width + LANES] = kb[rows, cols, width : width + LANES]

    def unpack(rows, cols):
        vb[rows, cols] = pltpu.roll(kb[rows, cols, 0:width].astype(jnp.float32), 4, 1).astype(jnp.bfloat16)

    def strip(source, rows, cols, send, recv, target):
        return pltpu.make_async_remote_copy(
            src_ref=source,
            dst_ref=kb.at[rows, cols],
            send_sem=send,
            recv_sem=recv,
            device_id=target,
            device_id_type=MESH,
        )

    right = {"col": lax.rem(col + 1, col_count)}
    left = {"col": lax.rem(col + col_count - 1, col_count)}
    down = {"row": lax.rem(row + 1, row_count)}
    up = {"row": lax.rem(row + row_count - 1, row_count)}
    has = {
        "right": col < col_count - 1, "left": col > 0, "down": row < row_count - 1, "up": row > 0,
    }
    left_strip, right_strip = pl.ds(0, UNIT), pl.ds(tile_cols + UNIT, UNIT)
    own_first, own_last = pl.ds(UNIT, UNIT), pl.ds(tile_cols, UNIT)
    all_cols = pl.ds(0, tile_cols)
    top_halo, bottom_halo = pl.ds(0, RADIUS), pl.ds(low + RADIUS, RADIUS)
    to_right = [strip(pack_cols.at[0], own_rows, left_strip, col_send.at[0], col_recv.at[0], right)]
    to_left = [strip(pack_cols.at[1], own_rows, right_strip, col_send.at[1], col_recv.at[1], left)]
    to_down = halo(pl.ds(tile_rows - RADIUS, RADIUS), all_cols, top_halo, core_cols, row_send.at[0], row_recv.at[0], down)
    to_up = halo(pl.ds(0, RADIUS), all_cols, bottom_halo, core_cols, row_send.at[1], row_recv.at[1], up)

    def start(copies):
        for copy in copies:
            copy.start()

    def got(copies):
        for copy in copies:
            copy.wait_recv()

    def sent(copies):
        for copy in copies:
            copy.wait_send()

    corners = []
    for index, (rows, row_side) in enumerate(((top_halo, "up"), (bottom_halo, "down"))):
        for way, (side, other, source, landing, neighbour) in enumerate(
            (("right", "left", own_last, left_strip, right), ("left", "right", own_first, right_strip, left))
        ):
            place = pack_cors.at[index, way]
            copy = strip(place, rows, landing, cor_send.at[index, way], cor_recv.at[index, way], neighbour)
            corners.append((copy, has[row_side] & has[side], has[row_side] & has[other], rows, source, landing, place, way == 1))

    def start_corner(copy, rows, source, place, leading):
        pack(rows, source, leading, place)
        copy.start()

    def got_corner(copy, rows, landing):
        copy.wait_recv()
        unpack(rows, landing)

    def got_strip(copies, landing):
        got(copies)
        unpack(own_rows, landing)

    def owner_of(unit):
        return lax.rem(unit * 5, tm_count)

    def unit_of(turn):
        return turn * tm_count + lax.rem(me * 13, tm_count)

    def place_of(unit):
        step = unit // half
        rest = unit - step * half
        central = rest < 2 * many
        past = rest - 2 * many
        pick = jnp.where(central, rest // many, past // few)
        inner = jnp.where(central, lax.rem(rest, many), lax.rem(past + few, few))
        block = jnp.where(step == 0, 1 + pick, 3 * pick)
        line = jnp.where(central, inner // middle, lax.rem(inner, RADIUS))
        group = jnp.where(central, 1 + lax.rem(inner, middle), (groups - 1) * (inner // RADIUS))
        return (block * RADIUS + line) * groups + group

    def first_copy(unit, owner):
        return pltpu.make_async_remote_copy(
            src_ref=ns.at[unit],
            dst_ref=nr.at[unit // tm_count, me],
            send_sem=p1_send,
            recv_sem=p1_recv.at[unit // tm_count],
            device_id={"tm": owner},
            device_id_type=MESH,
        )

    def second_copy(turn, unit, frame):
        return pltpu.make_async_remote_copy(
            src_ref=ts.at[turn, frame],
            dst_ref=out.at[place_of(unit)],
            send_sem=p2_send,
            recv_sem=p2_recv,
            device_id={"tm": frame},
            device_id_type=MESH,
        )

    def bias_of(live, marks):
        lane = lax.broadcasted_iota(jnp.int32, (UNIT, LANES), 1)
        pick = jnp.where(lane == 0, 1.0, 0.0).astype(jnp.bfloat16)
        keep = lax.dot_general(pick, live, (((1,), (1,)), ((), ())), preferred_element_type=jnp.float32)
        return jnp.where(marks[...] + keep[0:1] > 1.5, 0.0, NEG_FILL)

    def look(block, start_col, columns, bias, marks, target):
        first = block * RADIUS
        spread = columns + 2 * UNIT

        def fetch(kind, tile):
            lanes = slice(tile * LANES, (tile + 2) * LANES)
            if kind == 0:
                return qb[pl.ds(first, RADIUS), start_col : start_col + columns, lanes].reshape(RADIUS * columns, 2 * LANES)
            buffer = kb if kind == 1 else vb
            return buffer[pl.ds(first, span), start_col : start_col + spread, lanes].reshape(span * spread, 2 * LANES)

        live = kb[pl.ds(first, span), start_col : start_col + spread, width : width + LANES].reshape(span * spread, LANES)
        bias[...] = bias_of(live, marks)
        attend(fetch, bias, windows, size, target)

    def emit(start_unit, count, base, heads):
        stream = base.astype(jnp.float32) + jnp.dot(
            heads.astype(jnp.bfloat16), wo[...], preferred_element_type=jnp.float32
        )
        average = jnp.mean(stream, -1, keepdims=True)
        centered = stream - average
        variance = jnp.mean(centered * centered, -1, keepdims=True)
        normed = centered * lax.rsqrt(variance + EPSILON) * (1.0 + mo[1:2]) + mo[0:1]
        ns[pl.ds(start_unit, count)] = normed.astype(jnp.bfloat16).reshape(count, UNIT, width)

        def ahead(owner):
            return lax.rem(owner * 13 - start_unit + 4 * tm_count, tm_count)

        for offset in far_first(tm_count):
            owner = lax.rem(me + offset, tm_count)

            @pl.when(ahead(owner) < count)
            def _(owner=owner):
                first_copy(start_unit + ahead(owner), owner).start()

        @pl.when(ahead(me) < count)
        def _():
            unit = start_unit + ahead(me)
            nr[unit // tm_count, me] = ns[unit]

    def temporal(turn):
        unit = unit_of(turn)

        @pl.when(unit < units)
        def _():
            arrived = nr.at[turn, pl.ds(0, tm_count - 1)]
            pltpu.make_async_copy(arrived, arrived, p1_recv.at[turn]).wait()
            rows = nr[turn].reshape(tm_count * UNIT, width)
            for part in range(9):
                place = slice(part * 3 * LANES, (part + 1) * 3 * LANES)
                tq[:, place] = jnp.dot(
                    rows, wq[:, place], preferred_element_type=jnp.float32
                ).astype(jnp.bfloat16)

            def fetch(kind, tile):
                return tq[:, kind * width + tile * LANES : kind * width + (tile + 2) * LANES]

            attend(fetch, tbias, windows, size, tb)
            ts[turn] = tb[...].astype(jnp.bfloat16).reshape(tm_count, UNIT, width)
            pltpu.make_async_copy(ts.at[turn, me], out.at[place_of(unit)], own_sem.at[turn]).start()

            for offset in far_first(tm_count):
                second_copy(turn, unit, lax.rem(me + offset, tm_count)).start()

    for load in loads[4:7]:
        load.start()
    loads[1].wait()
    eye_shape = (tile_rows, tile_cols, tile_cols)
    diagonal = lax.broadcasted_iota(jnp.int32, eye_shape, 1) == lax.broadcasted_iota(jnp.int32, eye_shape, 2)
    spread_keep = jnp.where(diagonal, kk[...].astype(jnp.float32), 0.0).reshape(tile_rows * tile_cols, tile_cols)
    along = jnp.dot(
        spread_keep.astype(jnp.bfloat16),
        jnp.ones((tile_cols, LANES), jnp.bfloat16),
        preferred_element_type=jnp.float32,
    ).astype(jnp.bfloat16).reshape(tile_rows, tile_cols, LANES)
    flags[...] = along
    kb[own_rows, UNIT : UNIT + tile_cols, width : width + LANES] = along
    for index in (0, 2, 3):
        loads[index].wait()
    pack(own_rows, own_last, False, pack_cols.at[0])
    pack(own_rows, own_first, True, pack_cols.at[1])
    look(1, UNIT, middle * UNIT, cbias, cwin, hb)
    pl.semaphore_wait(barrier, tm_count - 1 + 4)
    pl.when(has["right"])(lambda: start(to_right))
    pl.when(has["left"])(lambda: start(to_left))
    pl.when(has["down"])(lambda: start(to_down))
    pl.when(has["up"])(lambda: start(to_up))
    loads[7].start()

    def step_body(step, carry):
        @pl.when(step == 1)
        def _():
            pl.when(has["up"])(lambda: got(to_down))
            pl.when(has["down"])(lambda: got(to_up))
            for copy, sends, _, rows, source, _, place, leading in corners:
                pl.when(sends)(
                    lambda copy=copy, rows=rows, source=source, place=place, leading=leading: start_corner(
                        copy, rows, source, place, leading
                    )
                )

        def centre(pick, carry):
            block = jnp.where(step == 0, 1 + pick, 3 * pick)
            pl.when(step + pick > 0)(lambda: look(block, UNIT, middle * UNIT, cbias, cwin, hb))

            @pl.when((step == 0) & (pick == 0))
            def _():
                for load in loads[4:7]:
                    load.wait()

            rows = middle * UNIT * RADIUS
            base = rb[pl.ds(block * RADIUS, RADIUS), UNIT : (middle + 1) * UNIT].reshape(rows, width)
            emit(step * half + pick * many, many, base, hb[...])
            return carry

        lax.fori_loop(0, 2, centre, 0)

        @pl.when(step == 0)
        def _():
            pl.when(has["left"])(lambda: got_strip(to_right, left_strip))
            pl.when(has["right"])(lambda: got_strip(to_left, right_strip))

        @pl.when(step == 1)
        def _():
            for copy, _, receives, rows, _, landing, _, _ in corners:
                pl.when(receives)(lambda copy=copy, rows=rows, landing=landing: got_corner(copy, rows, landing))

        def edge(pick, carry):
            block = jnp.where(step == 0, 1 + pick, 3 * pick)
            look(block, 0, UNIT, ebias, ewin, he.at[0])
            look(block, tile_cols - UNIT, UNIT, ebias, ewin, he.at[1])
            rows = UNIT * RADIUS
            lines = pl.ds(block * RADIUS, RADIUS)
            base = jnp.concatenate(
                [rb[lines, 0:UNIT].astype(jnp.float32).reshape(rows, width),
                 rb[lines, tile_cols - UNIT : tile_cols].astype(jnp.float32).reshape(rows, width)], 0
            )
            emit(step * half + 2 * many + pick * few, few, base, he[...].reshape(2 * rows, width))
            return carry

        lax.fori_loop(0, 2, edge, 0)
        pl.when(step == 0)(lambda: loads[7].wait())

        def turns(index, carry):
            temporal(index)
            return carry

        lax.fori_loop(step, 1 + step * (rounds - 1), turns, 0)
        return carry

    lax.fori_loop(0, 2, step_body, 0)

    pl.when(has["right"])(lambda: sent(to_right))
    pl.when(has["left"])(lambda: sent(to_left))
    pl.when(has["down"])(lambda: sent(to_down))
    pl.when(has["up"])(lambda: sent(to_up))
    for copy, sends, *_ in corners:
        pl.when(sends)(lambda copy=copy: copy.wait_send())

    def settle(own):
        away = pl.ds(0, units - own)
        pltpu.make_async_copy(ns.at[away], ns.at[away], p1_send).wait()
        for turn in range(own):
            pltpu.make_async_copy(ts.at[turn, me], out.at[place_of(unit_of(turn))], own_sem.at[turn]).wait()
        spent = ts.at[pl.ds(0, own), pl.ds(0, tm_count - 1)]
        pltpu.make_async_copy(spent, spent, p2_send).wait()
        pltpu.make_async_copy(out.at[away], out.at[away], p2_recv).wait()

    pl.when(unit_of(rounds - 1) < units)(lambda: settle(rounds))
    pl.when(unit_of(rounds - 1) >= units)(lambda: settle(rounds - 1))


def per_device(resid, spatial_qkv, key_keep, w_spatial_out, modulation, w_temporal_qkv):
    frame_count, tile_rows, tile_cols, width = resid.shape
    tm_count = lax.axis_size("tm")
    units = tile_rows * tile_cols // UNIT
    rounds = -(-units // tm_count)
    columns = tile_cols - 2 * UNIT
    core_rows, edge_rows = RADIUS * columns, RADIUS * UNIT
    core_keys, edge_keys = 3 * RADIUS * tile_cols, 3 * RADIUS * 3 * UNIT
    wide = tile_cols + 2 * UNIT
    pad_rows = tile_rows + 2 * RADIUS
    bf16, f32 = jnp.bfloat16, jnp.float32
    dma = pltpu.SemaphoreType.DMA
    result = pl.pallas_call(
        block_kernel,
        out_shape=jax.ShapeDtypeStruct((units, UNIT, width), bf16),
        in_specs=[pl.BlockSpec(memory_space=pltpu.HBM)] * 6,
        out_specs=pl.BlockSpec(memory_space=pl.ANY),
        scratch_shapes=[
            pltpu.VMEM((tile_rows, 1, tile_cols), jnp.int32),
            pltpu.VMEM((tile_rows, tile_cols, LANES), bf16),
            pltpu.VMEM((2, tile_rows, UNIT, width + LANES), bf16),
            pltpu.VMEM((2, 2, RADIUS, UNIT, width + LANES), bf16),
            pltpu.VMEM((pad_rows, wide, width + LANES), bf16),
            pltpu.VMEM((pad_rows, wide, width), bf16),
            pltpu.VMEM((tile_rows, tile_cols, width), bf16),
            pltpu.VMEM((tile_rows, tile_cols, width), bf16),
            pltpu.VMEM((width, width), bf16),
            pltpu.VMEM((2, width), f32),
            pltpu.VMEM((width, 3 * width), bf16),
            pltpu.VMEM((core_rows, width), f32),
            pltpu.VMEM((2, edge_rows, width), f32),
            pltpu.VMEM((core_rows, core_keys), f32),
            pltpu.VMEM((core_rows, core_keys), f32),
            pltpu.VMEM((edge_rows, edge_keys), f32),
            pltpu.VMEM((edge_rows, edge_keys), f32),
            pltpu.VMEM((units, UNIT, width), bf16),
            pltpu.VMEM((rounds, tm_count, UNIT, width), bf16),
            pltpu.VMEM((tm_count * UNIT, 3 * width), bf16),
            pltpu.VMEM((tm_count * UNIT, width), f32),
            pltpu.VMEM((tm_count * UNIT, tm_count * UNIT), f32),
            pltpu.VMEM((rounds, tm_count, UNIT, width), bf16),
            dma((8,)),
            dma((2,)), dma((2,)), dma((2, 3)), dma((2, 3)), dma((2, 2)), dma((2, 2)),
            dma, dma((rounds,)), dma, dma, dma((rounds,)),
        ],
        compiler_params=pltpu.CompilerParams(
            collective_id=0, has_side_effects=True, vmem_limit_bytes=58 * 1024 * 1024
        ),
    )(
        spatial_qkv.reshape(3, tile_rows, tile_cols, width),
        key_keep.reshape(tile_rows, 1, tile_cols),
        resid.reshape(tile_rows, tile_cols, width),
        w_spatial_out,
        modulation,
        w_temporal_qkv,
    )
    return result.reshape(frame_count, tile_rows, tile_cols, width)


def solution(mesh):
    return jax.shard_map(
        per_device,
        mesh=mesh,
        in_specs=(
            P("tm", "row", "col", None),
            P(None, "tm", "row", "col", None),
            P("tm", "row", "col"),
            P(),
            P(),
            P(),
        ),
        out_specs=P("tm", "row", "col", None),
        check_vma=False,
    )
```
